32 devices in a mesh: dp: 4 (over y, core), ctx: 8 (over z, x).
Axes of the slice: x: 2, y: 2, z: 4, core: 2. Of those that a mesh axis runs over, the one named last changes fastest.
Arguments:
- queries: bfloat16 [4096, 2048], P(('dp', 'ctx')), may hold values from -6 to 6
- key_rows: bfloat16 [4096, 2048], P(('dp', 'ctx')), may hold values from -6 to 6
- value_rows: bfloat16 [4096, 2048], P(('dp', 'ctx')), may hold values from -6 to 6
- hidden_in: bfloat16 [4096, 2304], P(('dp', 'ctx')), may hold values from -6 to 6
- beta_weight: bfloat16 [2304, 16], replicated, may hold values from -0.125 to 0.125
- log_gate: float32 [16, 4096], P(None, ('dp', 'ctx')), may hold values from -1 to 0
- out_grad: bfloat16 [4096, 2048], P(('dp', 'ctx')), may hold values from -24 to 24
- lengths: int32 [4, 4], P('dp'), may hold values from 1 to 512, 1024 in all within a row
- rewards: float32 [16], replicated, may hold values from -6 to 6
- prompts: int32 [16], replicated, may hold values from 0 to 3
Outputs:
- query_grad: bfloat16 [4096, 2048], P(('dp', 'ctx'))
- key_grad: bfloat16 [4096, 2048], P(('dp', 'ctx'))
- value_grad: bfloat16 [4096, 2048], P(('dp', 'ctx'))
- gate_grad: float32 [16, 4096], P(None, ('dp', 'ctx'))
- beta_weight_grad: float32 [2304, 16], P(('dp', 'ctx'))
The draws below stay inside these ranges and needn't reach their ends.
Inputs may be any that keep to these rules, and one draw needn't show every extreme that they name: `lengths`: each row sums to 1024; its largest entry is exactly 512.
All inputs are finite; a program needn't handle non-finite values.
Results may differ from the reference program's by a relative error of at most 0.001.
Values sent between devices are 32-bit elements; how exact they have to be, the bound alone decides.
A program may use at most 128 MiB of HBM per device.

```python
import math
import jax
import jax.numpy as jnp
import numpy as np
from jax import lax

D = 2304
HALF_HEADS = 16
HEAD_DIM = 128
BLOCK = 64
TOK_DEV = 128
ROLL = 4
GROUP_TOKENS = 1024
TOTAL_TOKENS = 4096
ROLLOUTS = 16
PROMPTS = 4
N_DP = 4


def draw_log_gate(key, part):
    key_vectors = jax.random.split(key, 7)
    fast_share = 0.5
    fast = jax.random.uniform(key_vectors[0], (HALF_HEADS, 1)) < fast_share
    fast_rate = jnp.exp(jax.random.uniform(key_vectors[1], (HALF_HEADS, 1), minval=math.log(1.0 / 50.0), maxval=math.log(1.0 / 30.0)))
    slow_rate = jnp.exp(jax.random.uniform(key_vectors[2], (HALF_HEADS, 1), minval=math.log(0.05), maxval=math.log(0.3))) / GROUP_TOKENS
    decay_speed = jnp.where(fast, fast_rate, slow_rate)
    block_multiplier = jnp.exp(jax.random.uniform(key_vectors[3], (HALF_HEADS, TOTAL_TOKENS // TOK_DEV, 1), minval=math.log(0.5), maxval=math.log(2.0)))
    block_multiplier = jnp.broadcast_to(block_multiplier, (HALF_HEADS, TOTAL_TOKENS // TOK_DEV, TOK_DEV)).reshape(HALF_HEADS, TOTAL_TOKENS)
    token_multiplier = jnp.exp(jax.random.uniform(key_vectors[4], (HALF_HEADS, TOTAL_TOKENS), minval=math.log(0.5), maxval=math.log(2.0)))
    spike_position = jax.random.uniform(key_vectors[5], (1, TOTAL_TOKENS)) < 3.0 / GROUP_TOKENS
    spike_magnitude = jax.random.uniform(key_vectors[6], (HALF_HEADS, TOTAL_TOKENS), minval=math.log(0.5), maxval=math.log(0.8))
    return (-decay_speed * block_multiplier * token_multiplier + jnp.where(spike_position, spike_magnitude, 0.0)).astype(jnp.float32)


def plant(entries, own_key, low, high):
    longest = entries.shape.index(max(entries.shape))
    spots = []
    for shift in (0, 1):
        where = [jax.random.randint(jax.random.fold_in(own_key, axis), (), 0, length) for axis, length in enumerate(entries.shape)]
        where[longest] = (where[longest] + shift) % entries.shape[longest]
        spots.append(tuple(where))
    return entries.at[spots[0]].set(low).at[spots[1]].set(high)


def with_spikes(array, key, source, target, shards_of, factor):
    owner, partner = [(jnp.arange(array.shape[position]) // (array.shape[position] // shards_of)).reshape([-1 if axis == position else 1 for axis in range(array.ndim)]) for position in (source, target)]
    chosen = jax.random.permutation(key, shards_of)[partner]
    strong = (owner == chosen) | (owner == (partner + shards_of // 2) % shards_of)
    return jnp.where(strong, factor * array, array)


def block_levels(stream_key, shape, cuts, low, high):
    loudness, own = 1.0, jax.random.fold_in(stream_key, 6)
    for position, shards_of in cuts:
        heights = jnp.exp(jax.random.uniform(jax.random.fold_in(own, position), (shards_of,), jnp.float32, low / len(cuts), high / len(cuts)))
        loudness = loudness * jnp.repeat(heights, shape[position] // shards_of).reshape([-1 if axis == position else 1 for axis in range(len(shape))])
    return loudness


def split_up(count, total, bound, skew):
    weights = [(1 << 20) // math.isqrt(rank ** skew) + 1 for rank in range(2, count + 1)]
    surplus, holding = total - bound - (count - 1), [1] * (count - 1)
    while surplus > 0:
        movable = [i for i in range(count - 1) if holding[i] < bound]
        pool, left = sum([weights[i] for i in movable]), surplus
        for i in movable:
            extra = min(bound - holding[i], max(1, left * weights[i] // pool), surplus)
            holding[i] = holding[i] + extra
            surplus = surplus - extra
    return np.array([bound] + holding)


def ragged(own_key, number_of, total, limit, lean):
    if number_of == 2:
        one = jax.random.randint(own_key, (), max(1, total - limit), min(limit, total - 1) + 1)
        return jnp.stack([one, total - one])
    sizes = jnp.asarray(split_up(number_of, total, limit, lean), jnp.int32)
    twos = (number_of - 1) // 2
    donor, taker = sizes[1:1 + 2 * twos:2], sizes[2:2 + 2 * twos:2]
    slack = jnp.minimum(donor - 1, limit - taker)
    shifted = jax.random.randint(jax.random.fold_in(own_key, 1), (twos,), 0, 1 << 20) % (slack + 1)
    sizes = sizes.at[1:1 + 2 * twos:2].set(donor - shifted).at[2:2 + 2 * twos:2].set(taker + shifted)
    return sizes[jax.random.permutation(jax.random.fold_in(own_key, 2), number_of)]


def gaussian(key, dims, scale, reach, cuts=(), held_as=jnp.bfloat16):
    drawn = jax.random.normal(key, dims, jnp.float32) * scale
    if len(cuts) > 0:
        drawn = block_levels(key, dims, cuts, -0.22, 0.18) * drawn
    return jnp.clip(drawn, min=-reach, max=reach).astype(held_as)


def bell_draw_with(rng, shape, scale, reach, cuts, heavy, kind=jnp.bfloat16):
    values = scale * jax.random.normal(rng, shape, jnp.float32)
    if cuts:
        values = values * block_levels(rng, shape, cuts, -0.22, 0.18)
    return jnp.clip(with_spikes(values, jax.random.fold_in(rng, 3), *heavy), -reach, reach).astype(kind)


def setup_inputs(seed: int = 0) -> dict:
    seeds = jax.random.split(jax.random.key(seed), 11)
    return {
        "queries": gaussian(seeds[0], (TOTAL_TOKENS, HALF_HEADS * HEAD_DIM), 1.0, 6.0, ((0, 32),)),
        "key_rows": gaussian(seeds[1], (TOTAL_TOKENS, HALF_HEADS * HEAD_DIM), 1.0, 6.0, ((0, 32),)),
        "value_rows": gaussian(seeds[2], (TOTAL_TOKENS, HALF_HEADS * HEAD_DIM), 1.0, 6.0, ((0, 32),)),
        "hidden_in": bell_draw_with(seeds[3], (TOTAL_TOKENS, D), 1.0, 6.0, ((0, 32),), (0, 1, 32, 2.75)),
        "beta_weight": gaussian(seeds[4], (D, HALF_HEADS), D ** -0.5, 0.125),
        "log_gate": draw_log_gate(jax.random.fold_in(seeds[10], 71), 0),
        "out_grad": gaussian(seeds[6], (TOTAL_TOKENS, HALF_HEADS * HEAD_DIM), 4.0, 24.0, ((0, 32),)),
        "lengths": jax.vmap(lambda own: ragged(own, ROLL, GROUP_TOKENS, GROUP_TOKENS // 2, 2))(jax.random.split(seeds[7], N_DP)).reshape((N_DP, ROLL)).astype(jnp.int32),
        "rewards": gaussian(seeds[8], (ROLLOUTS,), 1.0, 6.0, (), jnp.float32),
        "prompts": plant(jax.random.randint(seeds[9], (ROLLOUTS,), 0, PROMPTS), jax.random.fold_in(seeds[9], 1), 0, PROMPTS - 1).astype(jnp.int32),
    }


highest = lax.Precision.HIGHEST

def unit_rows(rows):
    return rows * lax.rsqrt(lax.optimization_barrier(jnp.sum(rows * rows, axis=-1, keepdims=True)) + 1e-06)

def unit_inverse(lower_part):
    size = lower_part.shape[-1]
    nilpotent = -lower_part
    total = jnp.eye(size, dtype=jnp.float32) + nilpotent
    power = nilpotent
    for level in range(max(1, (size - 1).bit_length()) - 1):
        power = jnp.einsum('nhij,nhjk->nhik', power, power, precision=highest)
        total = total + jnp.einsum('nhij,nhjk->nhik', total, power, precision=highest)
    return total

def block_terms(queries, key_rows, value_rows, beta, gate_log, starts):
    size = queries.shape[2]
    row_ids = lax.broadcasted_iota(jnp.int32, (size, size), 0)
    col_ids = lax.broadcasted_iota(jnp.int32, (size, size), 1)
    gamma = jnp.cumsum(gate_log, axis=-1)
    count = jnp.cumsum(starts, axis=-1)
    linked = (count[:, :, None] == count[:, None, :]) & (row_ids >= col_ids)
    linked = linked[:, None, :, :]
    spread = gamma[..., :, None] - gamma[..., None, :]
    decay = jnp.where(linked, jnp.exp(jnp.where(linked, spread, 0.0)), 0.0)
    head_decay = jnp.where(count == 0.0, 1.0, 0.0)[:, None, :] * jnp.exp(gamma)
    tail_decay = decay[..., size - 1, :]
    key_key = jnp.einsum('nhik,nhjk->nhij', key_rows, key_rows, precision=highest)
    lower_part = jnp.where(row_ids > col_ids, beta[..., :, None] * decay * key_key, 0.0)
    inverse = unit_inverse(lower_part)
    rhs_value = beta[..., None] * value_rows
    rhs_key = (beta * head_decay)[..., None] * key_rows
    u_zero = jnp.einsum('nhij,nhjv->nhiv', inverse, rhs_value, precision=highest)
    z_rows = jnp.einsum('nhij,nhjk->nhik', inverse, rhs_key, precision=highest)
    mixing = decay * jnp.einsum('nhik,nhjk->nhij', queries, key_rows, precision=highest)
    out_zero = jnp.einsum('nhij,nhjv->nhiv', mixing, u_zero, precision=highest)
    carry_q = head_decay[..., None] * queries - jnp.einsum('nhij,nhjk->nhik', mixing, z_rows, precision=highest)
    weighted = tail_decay[..., None] * key_rows
    state_zero = jnp.einsum('nhcv,nhck->nhvk', u_zero, weighted, precision=highest)
    identity = jnp.eye(key_rows.shape[-1], dtype=jnp.float32)
    transfer = head_decay[..., size - 1][..., None, None] * identity - jnp.einsum('nhck,nhcj->nhkj', z_rows, weighted, precision=highest)
    return (out_zero, carry_q, state_zero, transfer)

def run_blocks(out_zero, carry_q, state_zero, transfer, state_in):

    def advance(state, pieces):
        piece_out, piece_q, piece_state, piece_map = pieces
        result = piece_out + jnp.einsum('hck,hvk->hcv', piece_q, state, precision=highest)
        updated = jnp.einsum('hvk,hkj->hvj', state, piece_map, precision=highest) + piece_state
        return (updated, result)
    final, outputs = lax.scan(advance, state_in, (out_zero, carry_q, state_zero, transfer))
    return (outputs, final)

def segment_terms(query_f, key_f, value_f, logits, gate_log, starts):
    token_count, heads = logits.shape
    blocks = token_count // BLOCK

    def split(rows):
        return rows.reshape(blocks, BLOCK, heads, -1).transpose(0, 2, 1, 3)
    beta = jax.nn.sigmoid(logits).reshape(blocks, BLOCK, heads).transpose(0, 2, 1)
    gates = gate_log.reshape(heads, blocks, BLOCK).transpose(1, 0, 2)
    return block_terms(unit_rows(split(query_f)), unit_rows(split(key_f)), split(value_f), beta, gates, starts.reshape(blocks, BLOCK))

def output_from_terms(terms, state_in):
    outputs, final = run_blocks(terms[0], terms[1], terms[2], terms[3], state_in)
    token_count = outputs.shape[0] * outputs.shape[2]
    return (outputs.transpose(0, 2, 1, 3).reshape(token_count, -1), final)

def segment_output(query_f, key_f, value_f, logits, gate_log, starts, state_in):
    return output_from_terms(segment_terms(query_f, key_f, value_f, logits, gate_log, starts), state_in)

def token_plan(row_lengths, positions):
    ends = jnp.cumsum(row_lengths)
    begins = ends - row_lengths
    starts = jnp.any(positions[:, None] == begins[None, :], axis=1).astype(jnp.float32)
    member = ((positions[:, None] >= begins[None, :]) & (positions[:, None] < ends[None, :])).astype(jnp.float32)
    return (starts, member)

def advantages(rewards, prompts):
    same = (prompts[:, None] == prompts[None, :]).astype(jnp.float32)
    return rewards - lax.optimization_barrier(jnp.sum(same * rewards[None, :], axis=1)) / lax.optimization_barrier(jnp.sum(same, axis=1))

def reference(queries, key_rows, value_rows, hidden_in, beta_weight, log_gate, out_grad, lengths, rewards, prompts):
    roll_weight = advantages(rewards, prompts).reshape(N_DP, ROLL) * GROUP_TOKENS / (ROLL * lengths.astype(jnp.float32))
    positions = jnp.arange(GROUP_TOKENS, dtype=jnp.int32)
    starts, member = jax.vmap(token_plan, (0, None))(lengths, positions)
    token_weight = lax.optimization_barrier(jnp.sum(member * roll_weight[:, None, :], axis=-1)).reshape(TOTAL_TOKENS)
    cotangent = out_grad.astype(jnp.float32) * token_weight[:, None]
    logits = jnp.dot(hidden_in, beta_weight, preferred_element_type=jnp.float32)
    width = HALF_HEADS * HEAD_DIM
    zero_state = jnp.zeros((HALF_HEADS, HEAD_DIM, HEAD_DIM), jnp.float32)

    def one_group(pieces):
        query_f, key_f, value_f, group_logits, group_gates, group_starts, group_cot = pieces

        def forward(a_rows, b_rows, c_rows, d_rows, e_rows):
            return segment_output(a_rows, b_rows, c_rows, d_rows, e_rows, group_starts, zero_state)[0]
        primal, backward = jax.vjp(forward, query_f, key_f, value_f, group_logits, group_gates)
        return backward(group_cot)
    grads = lax.map(one_group, (queries.astype(jnp.float32).reshape(N_DP, GROUP_TOKENS, width), key_rows.astype(jnp.float32).reshape(N_DP, GROUP_TOKENS, width), value_rows.astype(jnp.float32).reshape(N_DP, GROUP_TOKENS, width), logits.reshape(N_DP, GROUP_TOKENS, HALF_HEADS), log_gate.reshape(HALF_HEADS, N_DP, GROUP_TOKENS).transpose(1, 0, 2), starts, cotangent.reshape(N_DP, GROUP_TOKENS, width)))
    query_grad = grads[0].reshape(TOTAL_TOKENS, width).astype(jnp.bfloat16)
    key_grad = grads[1].reshape(TOTAL_TOKENS, width).astype(jnp.bfloat16)
    value_grad = grads[2].reshape(TOTAL_TOKENS, width).astype(jnp.bfloat16)
    logit_grad = grads[3].reshape(TOTAL_TOKENS, HALF_HEADS)
    gate_grad = grads[4].transpose(1, 0, 2).reshape(HALF_HEADS, TOTAL_TOKENS)
    beta_weight_grad = jnp.dot(hidden_in.astype(jnp.float32).T, logit_grad, precision=highest, preferred_element_type=jnp.float32)
    return (query_grad, key_grad, value_grad, gate_grad, beta_weight_grad)
```

```python
import functools

import jax
import jax.numpy as jnp
from jax import lax
from jax.experimental import pallas as pl
from jax.experimental.pallas import tpu as pltpu
from jax.sharding import PartitionSpec as P

PACK = 2
SMALL = 16
highest = lax.Precision.HIGHEST
MESH = pl.DeviceIdType.MESH
F32 = jnp.float32
BF16 = jnp.bfloat16


def split(x):
    hi = x.astype(BF16)
    return hi, (x - hi.astype(F32)).astype(BF16)


def left(x):
    return jnp.concatenate(split(x), axis=1)


def left_t(x):
    return jnp.concatenate(split(x), axis=0)


def right(x):
    row = jnp.concatenate(split(x), axis=1)
    return jnp.concatenate([row, row], axis=0)


def right_t(x):
    hi, lo = split(x)
    return jnp.concatenate(
        [jnp.concatenate([hi, hi], axis=1), jnp.concatenate([lo, lo], axis=1)], axis=0
    )


def contract(a, b, dims):
    out = lax.dot_general(a, b, ((dims[:1], dims[1:]), ((), ())), preferred_element_type=F32)
    half = out.shape[1] // 2
    return out[:, :half] + out[:, half:]


def mul(a, b):
    return contract(left(a), right(b), (1, 0))


def mul_t(a, b):
    return contract(left(a), right_t(b), (1, 1))


def t_mul(a, b):
    return contract(left_t(a), right(b), (0, 0))


def stack(*parts):
    return jnp.concatenate(parts, axis=0)


def row_sum(x):
    return jnp.sum(x, axis=1, keepdims=True)


def inverses(lows, rows, cols):
    size = lows[0].shape[0]
    eye = jnp.where(rows == cols, 1.0, 0.0)
    base = min(SMALL, size)
    same = (rows // base) == (cols // base)
    powers = [jnp.where(same, -low, 0.0) for low in lows]
    totals = [eye + power for power in powers]
    powers = [mul(power, power) for power in powers]
    reach = 2
    while reach * 2 < base:
        both = [mul(stack(t, p), p) for t, p in zip(totals, powers)]
        totals = [t + b[:size] for t, b in zip(totals, both)]
        powers = [b[size:] for b in both]
        reach *= 2
    totals = [t + mul(t, p) for t, p in zip(totals, powers)]
    while base < size:
        own = ((rows // (2 * base)) == (cols // (2 * base))) & ((rows // base) != (cols // base))
        parts = [jnp.where(own, low, 0.0) for low in lows]
        mids = [mul(t, part) for t, part in zip(totals, parts)]
        totals = [t - mul(m, t) for t, m in zip(totals, mids)]
        base *= 2
    return totals


def kernel(
    q_ref, k_ref, v_ref, o_ref, cols_ref, rows_ref,
    dq_ref, dk_ref, dv_ref, dgate_ref, dlogit_ref,
    inv_ref, mix_ref, dkk_ref, dec_ref, map_ref, fout_ref, bout_ref, fin_ref, bin_ref,
    fsend, frecv, bsend, brecv,
):
    tokens = q_ref.shape[0]
    groups = cols_ref.shape[0]
    width = fin_ref.shape[-1]
    count = lax.axis_size("ctx")
    seg = lax.axis_index("ctx")
    last = count - 1

    barrier = pltpu.get_barrier_semaphore()

    @pl.when(seg > 0)
    def _():
        pl.semaphore_signal(barrier, inc=1, device_id={"ctx": seg - 1}, device_id_type=MESH)

    @pl.when(seg < last)
    def _():
        pl.semaphore_signal(barrier, inc=1, device_id={"ctx": seg + 1}, device_id_type=MESH)

    pl.semaphore_wait(barrier, jnp.minimum(seg, 1) + jnp.minimum(last - seg, 1))

    def forward_copy(group):
        return pltpu.make_async_remote_copy(
            src_ref=fout_ref.at[group], dst_ref=fin_ref.at[group],
            send_sem=fsend.at[group], recv_sem=frecv.at[group],
            device_id={"ctx": seg + 1}, device_id_type=MESH,
        )

    def backward_copy(group):
        return pltpu.make_async_remote_copy(
            src_ref=bout_ref.at[group], dst_ref=bin_ref.at[group],
            send_sem=bsend.at[group], recv_sem=brecv.at[group],
            device_id={"ctx": seg - 1}, device_id_type=MESH,
        )

    rows = lax.broadcasted_iota(jnp.int32, (tokens, tokens), 0)
    cols = lax.broadcasted_iota(jnp.int32, (tokens, tokens), 1)
    heads = range(PACK)

    def lanes(group, i):
        return pl.ds(pl.multiple_of((group * PACK + i) * width, width), width)

    def load(ref, group, i):
        return ref[:, lanes(group, i)].astype(F32)

    def token_columns(group, i):
        block = cols_ref[group]
        row_block = rows_ref[group]
        beta = block[:, i:i + 1]
        gamma = block[:, PACK + i:PACK + i + 1]
        number = block[:, 2 * PACK:2 * PACK + 1]
        weight = block[:, 2 * PACK + 1:2 * PACK + 2]
        gamma_row = row_block[i:i + 1, :]
        number_row = row_block[PACK:PACK + 1, :]
        head = jnp.where(number == 0.0, jnp.exp(gamma), 0.0)
        tied = number == number_row[:, tokens - 1:tokens]
        tail = jnp.where(
            tied, jnp.exp(jnp.where(tied, gamma_row[:, tokens - 1:tokens] - gamma, 0.0)), 0.0
        )
        return beta, gamma, number, weight, gamma_row, number_row, head, tail

    def scales(x):
        return lax.rsqrt(row_sum(x * x) + 1e-06)

    def local_part(group):
        lows, keep = [], []
        for i in heads:
            beta, gamma, number, weight, gamma_row, number_row, head, tail = token_columns(group, i)
            q, k = load(q_ref, group, i), load(k_ref, group, i)
            qh, kh = q * scales(q), k * scales(k)
            linked = (number == number_row) & (rows >= cols)
            decay = jnp.where(linked, jnp.exp(jnp.where(linked, gamma - gamma_row, 0.0)), 0.0)
            both = mul_t(stack(kh, qh), kh)
            dkk = jnp.where(rows > cols, decay * both[:tokens], 0.0)
            mix = decay * both[tokens:]
            dec_ref[group, i] = decay
            dkk_ref[group, i] = dkk
            mix_ref[group, i] = mix
            lows.append(beta * dkk)
            keep.append((beta, weight, head, tail, qh, kh, mix))
        invs = inverses(lows, rows, cols)
        for i in heads:
            inv_ref[group, i] = invs[i]
        pairs = []
        for i in heads:
            beta, weight, head, tail, qh, kh, mix = keep[i]
            v = load(v_ref, group, i)
            pairs.append(mul(invs[i], jnp.concatenate([beta * v, (beta * head) * kh], axis=1)))
        eye = jnp.where(rows == cols, 1.0, 0.0)
        for i in heads:
            beta, weight, head, tail, qh, kh, mix = keep[i]
            z = pairs[i][:, width:]
            ends = t_mul(pairs[i], tail * kh)
            fout_ref[group, i] = ends[:width]
            map_ref[group, i] = head[tokens - 1:tokens, :] * eye - ends[width:]
            carry = head * qh - mul(mix, z)
            bout_ref[group, i] = t_mul(load(o_ref, group, i) * weight, carry)

    def forward_hop(group):
        @pl.when(seg == 0)
        def _():
            fin_ref[group] = jnp.zeros_like(fin_ref[group])

        @pl.when(seg > 0)
        def _():
            forward_copy(group).wait_recv()

        @pl.when((seg > 0) & (seg < last))
        def _():
            for i in heads:
                fout_ref[group, i] = fout_ref[group, i] + mul(fin_ref[group, i], map_ref[group, i])

        @pl.when(seg < last)
        def _():
            forward_copy(group).start()

    def backward_hop(group):
        @pl.when(seg == last)
        def _():
            bin_ref[group] = jnp.zeros_like(bin_ref[group])

        @pl.when(seg < last)
        def _():
            backward_copy(group).wait_recv()

        @pl.when((seg > 0) & (seg < last))
        def _():
            for i in heads:
                bout_ref[group, i] = bout_ref[group, i] + mul_t(bin_ref[group, i], map_ref[group, i])

        @pl.when(seg > 0)
        def _():
            backward_copy(group).start()

    def gradient_part(group):
        upper = jnp.where(rows < cols, 1.0, 0.0).astype(BF16)
        upper = stack(upper, upper)
        keep = []
        for i in heads:
            beta, gamma, number, weight, gamma_row, number_row, head, tail = token_columns(group, i)
            q, k = load(q_ref, group, i), load(k_ref, group, i)
            qs, ks = scales(q), scales(k)
            qh, kh = q * qs, k * ks
            state = fin_ref[group, i]
            both = mul_t(stack(qh, kh), state)
            keep.append((beta, weight, head, tail, qs, ks, qh, kh, state, both[:tokens], both[tokens:]))
        rests = [load(v_ref, group, i) - keep[i][2] * keep[i][10] for i in heads]
        us = [mul(inv_ref[group, i], keep[i][0] * rests[i]) for i in heads]
        dos = [load(o_ref, group, i) * keep[i][1] for i in heads]
        dus = [
            t_mul(mix_ref[group, i], dos[i]) + mul_t(keep[i][3] * keep[i][7], bin_ref[group, i])
            for i in heads
        ]
        drs = [t_mul(inv_ref[group, i], dus[i]) for i in heads]
        squares = [mul_t(stack(dos[i], drs[i]), us[i]) for i in heads]
        logit_columns = []
        for i in heads:
            beta, weight, head, tail, qs, ks, qh, kh, state, qstate, kstate = keep[i]
            u, do, dr, rest, after = us[i], dos[i], drs[i], rests[i], bin_ref[group, i]
            decay, dkk = dec_ref[group, i], dkk_ref[group, i]
            dmix = squares[i][:tokens]
            dlow = jnp.where(rows > cols, -squares[i][tokens:], 0.0)
            inward = mul(stack(head * do, (-beta * head) * dr), state)
            uafter = mul(u, after)
            da = dmix * decay
            dpair = dlow * (beta * decay)
            pairs = stack(da, dpair)
            direct = mul(pairs, kh)
            turned = t_mul(pairs, stack(qh, kh))
            dqh = inward[:tokens] + direct[:tokens]
            dkh = inward[tokens:] + direct[tokens:] + turned + tail * uafter
            dq_ref[:, lanes(group, i)] = (qs * (dqh - qh * row_sum(qh * dqh))).astype(BF16)
            dk_ref[:, lanes(group, i)] = (ks * (dkh - kh * row_sum(kh * dkh))).astype(BF16)
            dv_ref[:, lanes(group, i)] = (beta * dr).astype(BF16)
            lowpart = dlow * dkk
            spread = dmix * mix_ref[group, i] + beta * lowpart
            across = lax.dot_general(
                left(spread), upper, (((1,), (0,)), ((), ())), preferred_element_type=F32
            )
            total = jnp.sum(row_sum(after * state), axis=0, keepdims=True)
            headgrad = row_sum(do * qstate) - beta * row_sum(dr * kstate)
            headgrad = head * (headgrad + jnp.where(rows[:, :1] == tokens - 1, total, 0.0))
            tailgrad = tail * row_sum(kh * uafter)
            dgate_ref[group, i:i + 1, :] = jnp.sum(
                jnp.where(rows >= cols, across + headgrad, tailgrad), axis=0, keepdims=True
            )
            dbeta = row_sum(dr * rest) + row_sum(lowpart)
            logit_columns.append(dbeta * beta * (1.0 - beta))
        dlogit_ref[group] = jnp.concatenate(logit_columns, axis=1)

    def step(t, unused):
        @pl.when(t < groups)
        def _():
            local_part(t)

        f = t - seg

        @pl.when((f >= 0) & (f < groups))
        def _():
            forward_hop(f)

        b = t - (last - seg)

        @pl.when((b >= 0) & (b < groups))
        def _():
            backward_hop(b)

        @pl.when(t >= last)
        def _():
            gradient_part(t - last)

        return unused

    lax.fori_loop(0, groups + last, step, 0)

    def drain(group, unused):
        @pl.when(seg < last)
        def _():
            forward_copy(group).wait_send()

        @pl.when(seg > 0)
        def _():
            backward_copy(group).wait_send()

        return unused

    lax.fori_loop(0, groups, drain, 0)


def token_plan(row_lengths, positions):
    ends = jnp.cumsum(row_lengths)
    begins = ends - row_lengths
    starts = jnp.any(positions[:, None] == begins[None, :], axis=1).astype(jnp.float32)
    member = (
        (positions[:, None] >= begins[None, :]) & (positions[:, None] < ends[None, :])
    ).astype(jnp.float32)
    return (starts, member)


def advantages(rewards, prompts):
    same = (prompts[:, None] == prompts[None, :]).astype(jnp.float32)
    return rewards - jnp.sum(same * rewards[None, :], axis=1) / jnp.sum(same, axis=1)


def local(
    queries, key_rows, value_rows, hidden_in, beta_weight, log_gate, out_grad,
    lengths, rewards, prompts,
):
    tokens = queries.shape[0]
    heads = beta_weight.shape[1]
    width = queries.shape[1] // heads
    groups = heads // PACK
    ctx_count = lax.axis_size("ctx")
    roll_count = lengths.shape[1]
    group_tokens = tokens * ctx_count
    positions = lax.axis_index("ctx") * tokens + jnp.arange(tokens, dtype=jnp.int32)
    starts, member = token_plan(lengths[0], positions)
    own_advantage = lax.dynamic_slice_in_dim(
        advantages(rewards, prompts), lax.axis_index("dp") * roll_count, roll_count
    )
    roll_weight = own_advantage * group_tokens / (roll_count * lengths[0].astype(jnp.float32))
    token_weight = jnp.sum(member * roll_weight[None, :], axis=-1)
    logits = jnp.dot(hidden_in, beta_weight, preferred_element_type=jnp.float32)
    beta = jax.nn.sigmoid(logits)
    gamma = jnp.cumsum(log_gate, axis=-1)
    number = jnp.cumsum(starts)
    shared = jnp.broadcast_to(
        jnp.stack([number, token_weight], axis=1)[None], (groups, tokens, 2)
    )
    columns = jnp.concatenate(
        [
            beta.reshape(tokens, groups, PACK).transpose(1, 0, 2),
            gamma.reshape(groups, PACK, tokens).transpose(0, 2, 1),
            shared,
        ],
        axis=2,
    )
    lines = jnp.concatenate(
        [
            gamma.reshape(groups, PACK, tokens),
            jnp.broadcast_to(number[None, None], (groups, 1, tokens)),
        ],
        axis=1,
    )
    square = (groups, PACK, tokens, tokens)
    states = (groups, PACK, width, width)
    vmem = pl.BlockSpec(memory_space=pltpu.VMEM)
    dq, dk, dv, dgate, dlogit = pl.pallas_call(
        kernel,
        out_shape=(
            jax.ShapeDtypeStruct(queries.shape, BF16),
            jax.ShapeDtypeStruct(queries.shape, BF16),
            jax.ShapeDtypeStruct(queries.shape, BF16),
            jax.ShapeDtypeStruct((groups, PACK, tokens), F32),
            jax.ShapeDtypeStruct((groups, tokens, PACK), F32),
        ),
        in_specs=[vmem] * 6,
        out_specs=(vmem,) * 5,
        scratch_shapes=[pltpu.VMEM(square, F32)] * 4
        + [pltpu.VMEM(states, F32)] * 5
        + [pltpu.SemaphoreType.DMA((groups,))] * 4,
        compiler_params=pltpu.CompilerParams(
            collective_id=0, has_side_effects=True, vmem_limit_bytes=48 * 2**20
        ),
        name="delta_backward",
    )(queries, key_rows, value_rows, out_grad, columns, lines)
    logit_grad = dlogit.transpose(1, 0, 2).reshape(tokens, heads)
    piece = hidden_in.astype(jnp.float32)
    beta_weight_grad = lax.psum_scatter(
        jnp.dot(piece.T, logit_grad, precision=highest, preferred_element_type=jnp.float32),
        ("dp", "ctx"),
        scatter_dimension=0,
        tiled=True,
    )
    return (dq, dk, dv, dgate.reshape(heads, tokens), beta_weight_grad)


def solution(mesh):
    rows = P(("dp", "ctx"), None)
    in_specs = (
        rows, rows, rows, rows, P(), P(None, ("dp", "ctx")), rows, P("dp", None), P(), P(),
    )
    out_specs = (rows, rows, rows, P(None, ("dp", "ctx")), rows)
    return jax.shard_map(local, mesh=mesh, in_specs=in_specs, out_specs=out_specs, check_vma=False)
```

```python
import functools

import jax
import jax.numpy as jnp
from jax import lax
from jax.experimental import pallas as pl
from jax.experimental.pallas import tpu as pltpu
from jax.sharding import PartitionSpec as P

PACK = 2
SMALL = 16
MESH = pl.DeviceIdType.MESH
F32 = jnp.float32
BF16 = jnp.bfloat16


def split(x):
    hi = x.astype(BF16)
    return hi, (x - hi.astype(F32)).astype(BF16)


def left(x):
    return jnp.concatenate(split(x), axis=1)


def left_t(x):
    return jnp.concatenate(split(x), axis=0)


def right(x):
    row = jnp.concatenate(split(x), axis=1)
    return jnp.concatenate([row, row], axis=0)


def right_t(x):
    hi, lo = split(x)
    return jnp.concatenate(
        [jnp.concatenate([hi, hi], axis=1), jnp.concatenate([lo, lo], axis=1)], axis=0
    )


def contract(a, b, dims):
    out = lax.dot_general(a, b, ((dims[:1], dims[1:]), ((), ())), preferred_element_type=F32)
    half = out.shape[1] // 2
    return out[:, :half] + out[:, half:]


def mul(a, b):
    return contract(left(a), right(b), (1, 0))


def mul_t(a, b):
    return contract(left(a), right_t(b), (1, 1))


def t_mul(a, b):
    return contract(left_t(a), right(b), (0, 0))


def stack(*parts):
    return jnp.concatenate(parts, axis=0)


def row_sum(x):
    return jnp.sum(x, axis=1, keepdims=True)


def inverses(lows, rows, cols):
    size = lows[0].shape[0]
    eye = jnp.where(rows == cols, 1.0, 0.0)
    base = min(SMALL, size)
    same = (rows // base) == (cols // base)
    powers = [jnp.where(same, -low, 0.0) for low in lows]
    totals = [eye + power for power in powers]
    powers = [mul(power, power) for power in powers]
    reach = 2
    while reach * 2 < base:
        both = [mul(stack(t, p), p) for t, p in zip(totals, powers)]
        totals = [t + b[:size] for t, b in zip(totals, both)]
        powers = [b[size:] for b in both]
        reach *= 2
    totals = [t + mul(t, p) for t, p in zip(totals, powers)]
    while base < size:
        own = ((rows // (2 * base)) == (cols // (2 * base))) & ((rows // base) != (cols // base))
        parts = [jnp.where(own, low, 0.0) for low in lows]
        mids = [mul(t, part) for t, part in zip(totals, parts)]
        totals = [t - mul(m, t) for t, m in zip(totals, mids)]
        base *= 2
    return totals


def kernel(
    q_ref, k_ref, v_ref, o_ref, cols_ref, rows_ref, hidden_ref,
    dq_ref, dk_ref, dv_ref, dgate_ref, weight_ref,
    inv_ref, mix_ref, dkk_ref, dec_ref, map_ref, fout_ref, bout_ref, fin_ref, bin_ref,
    dlogit_ref, whole_ref, near_out, near_in, far_out, far_in,
    fsend, frecv, bsend, brecv, nsend, nrecv, wsend, wrecv,
):
    tokens = q_ref.shape[0]
    groups = cols_ref.shape[0]
    width = fin_ref.shape[-1]
    count = lax.axis_size("ctx")
    seg = lax.axis_index("ctx")
    last = count - 1

    barrier = pltpu.get_barrier_semaphore()

    part = lax.axis_index("dp")
    parts = lax.axis_size("dp")
    for by in range(1, count):
        pl.semaphore_signal(
            barrier, inc=1, device_id={"ctx": lax.rem(seg + by, count)}, device_id_type=MESH
        )
    for by in range(1, parts):
        pl.semaphore_signal(
            barrier, inc=1, device_id={"dp": lax.rem(part + by, parts)}, device_id_type=MESH
        )
    pl.semaphore_wait(barrier, count + parts - 2)

    def forward_copy(group):
        return pltpu.make_async_remote_copy(
            src_ref=fout_ref.at[group], dst_ref=fin_ref.at[group],
            send_sem=fsend.at[group], recv_sem=frecv.at[group],
            device_id={"ctx": seg + 1}, device_id_type=MESH,
        )

    def backward_copy(group):
        return pltpu.make_async_remote_copy(
            src_ref=bout_ref.at[group], dst_ref=bin_ref.at[group],
            send_sem=bsend.at[group], recv_sem=brecv.at[group],
            device_id={"ctx": seg - 1}, device_id_type=MESH,
        )

    rows = lax.broadcasted_iota(jnp.int32, (tokens, tokens), 0)
    cols = lax.broadcasted_iota(jnp.int32, (tokens, tokens), 1)
    heads = range(PACK)

    def lanes(group, i):
        return pl.ds(pl.multiple_of((group * PACK + i) * width, width), width)

    def load(ref, group, i):
        return ref[:, lanes(group, i)].astype(F32)

    def token_columns(group, i):
        block = cols_ref[group]
        row_block = rows_ref[group]
        beta = block[:, i:i + 1]
        gamma = block[:, PACK + i:PACK + i + 1]
        number = block[:, 2 * PACK:2 * PACK + 1]
        weight = block[:, 2 * PACK + 1:2 * PACK + 2]
        gamma_row = row_block[i:i + 1, :]
        number_row = row_block[PACK:PACK + 1, :]
        head = jnp.where(number == 0.0, jnp.exp(gamma), 0.0)
        tied = number == number_row[:, tokens - 1:tokens]
        tail = jnp.where(
            tied, jnp.exp(jnp.where(tied, gamma_row[:, tokens - 1:tokens] - gamma, 0.0)), 0.0
        )
        return beta, gamma, number, weight, gamma_row, number_row, head, tail

    def scales(x):
        return lax.rsqrt(row_sum(x * x) + 1e-06)

    def local_part(group):
        lows, keep = [], []
        for i in heads:
            beta, gamma, number, weight, gamma_row, number_row, head, tail = token_columns(group, i)
            q, k = load(q_ref, group, i), load(k_ref, group, i)
            qh, kh = q * scales(q), k * scales(k)
            linked = (number == number_row) & (rows >= cols)
            decay = jnp.where(linked, jnp.exp(jnp.where(linked, gamma - gamma_row, 0.0)), 0.0)
            both = mul_t(stack(kh, qh), kh)
            dkk = jnp.where(rows > cols, decay * both[:tokens], 0.0)
            mix = decay * both[tokens:]
            dec_ref[group, i] = decay
            dkk_ref[group, i] = dkk
            mix_ref[group, i] = mix
            lows.append(beta * dkk)
            keep.append((beta, weight, head, tail, qh, kh, mix))
        invs = inverses(lows, rows, cols)
        for i in heads:
            inv_ref[group, i] = invs[i]
        pairs = []
        for i in heads:
            beta, weight, head, tail, qh, kh, mix = keep[i]
            v = load(v_ref, group, i)
            pairs.append(mul(invs[i], jnp.concatenate([beta * v, (beta * head) * kh], axis=1)))
        eye = jnp.where(rows == cols, 1.0, 0.0)
        for i in heads:
            beta, weight, head, tail, qh, kh, mix = keep[i]
            z = pairs[i][:, width:]
            ends = t_mul(pairs[i], tail * kh)
            fout_ref[group, i] = ends[:width]
            map_ref[group, i] = head[tokens - 1:tokens, :] * eye - ends[width:]
            carry = head * qh - mul(mix, z)
            bout_ref[group, i] = t_mul(load(o_ref, group, i) * weight, carry)

    def forward_hop(group):
        @pl.when(seg == 0)
        def _():
            fin_ref[group] = jnp.zeros_like(fin_ref[group])

        @pl.when(seg > 0)
        def _():
            forward_copy(group).wait_recv()

        @pl.when((seg > 0) & (seg < last))
        def _():
            for i in heads:
                fout_ref[group, i] = fout_ref[group, i] + mul(fin_ref[group, i], map_ref[group, i])

        @pl.when(seg < last)
        def _():
            forward_copy(group).start()

    def backward_hop(group):
        @pl.when(seg == last)
        def _():
            bin_ref[group] = jnp.zeros_like(bin_ref[group])

        @pl.when(seg < last)
        def _():
            backward_copy(group).wait_recv()

        @pl.when((seg > 0) & (seg < last))
        def _():
            for i in heads:
                bout_ref[group, i] = bout_ref[group, i] + mul_t(bin_ref[group, i], map_ref[group, i])

        @pl.when(seg > 0)
        def _():
            backward_copy(group).start()

    def gradient_part(group):
        upper = jnp.where(rows < cols, 1.0, 0.0).astype(BF16)
        upper = stack(upper, upper)
        keep = []
        for i in heads:
            beta, gamma, number, weight, gamma_row, number_row, head, tail = token_columns(group, i)
            q, k = load(q_ref, group, i), load(k_ref, group, i)
            qs, ks = scales(q), scales(k)
            qh, kh = q * qs, k * ks
            state = fin_ref[group, i]
            both = mul_t(stack(qh, kh), state)
            keep.append((beta, weight, head, tail, qs, ks, qh, kh, state, both[:tokens], both[tokens:]))
        rests = [load(v_ref, group, i) - keep[i][2] * keep[i][10] for i in heads]
        us = [mul(inv_ref[group, i], keep[i][0] * rests[i]) for i in heads]
        dos = [load(o_ref, group, i) * keep[i][1] for i in heads]
        dus = [
            t_mul(mix_ref[group, i], dos[i]) + mul_t(keep[i][3] * keep[i][7], bin_ref[group, i])
            for i in heads
        ]
        drs = [t_mul(inv_ref[group, i], dus[i]) for i in heads]
        squares = [mul_t(stack(dos[i], drs[i]), us[i]) for i in heads]
        logit_columns = []
        for i in heads:
            beta, weight, head, tail, qs, ks, qh, kh, state, qstate, kstate = keep[i]
            u, do, dr, rest, after = us[i], dos[i], drs[i], rests[i], bin_ref[group, i]
            decay, dkk = dec_ref[group, i], dkk_ref[group, i]
            dmix = squares[i][:tokens]
            dlow = jnp.where(rows > cols, -squares[i][tokens:], 0.0)
            inward = mul(stack(head * do, (-beta * head) * dr), state)
            uafter = mul(u, after)
            da = dmix * decay
            dpair = dlow * (beta * decay)
            pairs = stack(da, dpair)
            direct = mul(pairs, kh)
            turned = t_mul(pairs, stack(qh, kh))
            dqh = inward[:tokens] + direct[:tokens]
            dkh = inward[tokens:] + direct[tokens:] + turned + tail * uafter
            dq_ref[:, lanes(group, i)] = (qs * (dqh - qh * row_sum(qh * dqh))).astype(BF16)
            dk_ref[:, lanes(group, i)] = (ks * (dkh - kh * row_sum(kh * dkh))).astype(BF16)
            dv_ref[:, lanes(group, i)] = (beta * dr).astype(BF16)
            lowpart = dlow * dkk
            spread = dmix * mix_ref[group, i] + beta * lowpart
            across = lax.dot_general(
                left(spread), upper, (((1,), (0,)), ((), ())), preferred_element_type=F32
            )
            total = jnp.sum(row_sum(after * state), axis=0, keepdims=True)
            headgrad = row_sum(do * qstate) - beta * row_sum(dr * kstate)
            headgrad = head * (headgrad + jnp.where(rows[:, :1] == tokens - 1, total, 0.0))
            tailgrad = tail * row_sum(kh * uafter)
            dgate_ref[group, i:i + 1, :] = jnp.sum(
                jnp.where(rows >= cols, across + headgrad, tailgrad), axis=0, keepdims=True
            )
            dbeta = row_sum(dr * rest) + row_sum(lowpart)
            logit_columns.append(dbeta * beta * (1.0 - beta))
        dlogit_ref[group] = jnp.concatenate(logit_columns, axis=1)

    def step(t, unused):
        @pl.when(t < groups)
        def _():
            local_part(t)

        f = t - seg

        @pl.when((f >= 0) & (f < groups))
        def _():
            forward_hop(f)

        b = t - (last - seg)

        @pl.when((b >= 0) & (b < groups))
        def _():
            backward_hop(b)

        @pl.when(t >= last)
        def _():
            gradient_part(t - last)

        return unused

    lax.fori_loop(0, groups + last, step, 0)

    def drain(group, unused):
        @pl.when(seg < last)
        def _():
            forward_copy(group).wait_send()

        @pl.when(seg > 0)
        def _():
            backward_copy(group).wait_send()

        return unused

    logit_grad = jnp.concatenate([dlogit_ref[g] for g in range(groups)], axis=1)
    hidden = hidden_ref[...]
    whole_ref[...] = lax.dot_general(
        left_t(logit_grad), stack(hidden, hidden), (((0,), (0,)), ((), ())),
        preferred_element_type=F32,
    )
    owned = near_out.shape[-1]
    for p in range(parts):
        for c in range(count):
            at = (p * count + c) * owned
            near_out[p, c] = whole_ref[:, at:at + owned]

    def near_copy(by):
        to = lax.rem(part + by, parts)
        return pltpu.make_async_remote_copy(
            src_ref=near_out.at[to], dst_ref=near_in.at[by - 1],
            send_sem=nsend.at[by - 1], recv_sem=nrecv.at[by - 1],
            device_id={"dp": to}, device_id_type=MESH,
        )

    def far_copy(by):
        to = lax.rem(seg + by, count)
        return pltpu.make_async_remote_copy(
            src_ref=far_out.at[to], dst_ref=far_in.at[by - 1],
            send_sem=wsend.at[by - 1], recv_sem=wrecv.at[by - 1],
            device_id={"ctx": to}, device_id_type=MESH,
        )

    for by in range(1, parts):
        near_copy(by).start()
    total = near_out[part]
    for by in range(1, parts):
        near_copy(by).wait_recv()
        total = total + near_in[by - 1]
    far_out[...] = total
    for by in range(1, count):
        far_copy(by).start()
    total = far_out[seg]
    for by in range(1, count):
        far_copy(by).wait_recv()
        total = total + far_in[by - 1]
    weight_ref[...] = total
    for by in range(1, parts):
        near_copy(by).wait_send()
    for by in range(1, count):
        far_copy(by).wait_send()

    lax.fori_loop(0, groups, drain, 0)


def token_plan(row_lengths, positions):
    ends = jnp.cumsum(row_lengths)
    begins = ends - row_lengths
    starts = jnp.any(positions[:, None] == begins[None, :], axis=1).astype(jnp.float32)
    member = (
        (positions[:, None] >= begins[None, :]) & (positions[:, None] < ends[None, :])
    ).astype(jnp.float32)
    return (starts, member)


def advantages(rewards, prompts):
    same = (prompts[:, None] == prompts[None, :]).astype(jnp.float32)
    return rewards - jnp.sum(same * rewards[None, :], axis=1) / jnp.sum(same, axis=1)


def local(
    queries, key_rows, value_rows, hidden_in, beta_weight, log_gate, out_grad,
    lengths, rewards, prompts,
):
    tokens = queries.shape[0]
    heads = beta_weight.shape[1]
    width = queries.shape[1] // heads
    groups = heads // PACK
    ctx_count = lax.axis_size("ctx")
    roll_count = lengths.shape[1]
    group_tokens = tokens * ctx_count
    positions = lax.axis_index("ctx") * tokens + jnp.arange(tokens, dtype=jnp.int32)
    starts, member = token_plan(lengths[0], positions)
    own_advantage = lax.dynamic_slice_in_dim(
        advantages(rewards, prompts), lax.axis_index("dp") * roll_count, roll_count
    )
    roll_weight = own_advantage * group_tokens / (roll_count * lengths[0].astype(jnp.float32))
    token_weight = jnp.sum(member * roll_weight[None, :], axis=-1)
    logits = jnp.dot(hidden_in, beta_weight, preferred_element_type=jnp.float32)
    beta = jax.nn.sigmoid(logits)
    gamma = jnp.cumsum(log_gate, axis=-1)
    number = jnp.cumsum(starts)
    shared = jnp.broadcast_to(
        jnp.stack([number, token_weight], axis=1)[None], (groups, tokens, 2)
    )
    columns = jnp.concatenate(
        [
            beta.reshape(tokens, groups, PACK).transpose(1, 0, 2),
            gamma.reshape(groups, PACK, tokens).transpose(0, 2, 1),
            shared,
        ],
        axis=2,
    )
    lines = jnp.concatenate(
        [
            gamma.reshape(groups, PACK, tokens),
            jnp.broadcast_to(number[None, None], (groups, 1, tokens)),
        ],
        axis=1,
    )
    square = (groups, PACK, tokens, tokens)
    states = (groups, PACK, width, width)
    vmem = pl.BlockSpec(memory_space=pltpu.VMEM)
    model = hidden_in.shape[1]
    dp_count = lax.axis_size("dp")
    owned = model // (dp_count * ctx_count)
    dq, dk, dv, dgate, own_grad = pl.pallas_call(
        kernel,
        out_shape=(
            jax.ShapeDtypeStruct(queries.shape, BF16),
            jax.ShapeDtypeStruct(queries.shape, BF16),
            jax.ShapeDtypeStruct(queries.shape, BF16),
            jax.ShapeDtypeStruct((groups, PACK, tokens), F32),
            jax.ShapeDtypeStruct((heads, owned), F32),
        ),
        in_specs=[vmem] * 7,
        out_specs=(vmem,) * 5,
        scratch_shapes=[pltpu.VMEM(square, F32)] * 4
        + [pltpu.VMEM(states, F32)] * 5
        + [
            pltpu.VMEM((groups, tokens, PACK), F32),
            pltpu.VMEM((heads, model), F32),
            pltpu.VMEM((dp_count, ctx_count, heads, owned), F32),
            pltpu.VMEM((dp_count - 1 or 1, ctx_count, heads, owned), F32),
            pltpu.VMEM((ctx_count, heads, owned), F32),
            pltpu.VMEM((ctx_count - 1, heads, owned), F32),
        ]
        + [pltpu.SemaphoreType.DMA((groups,))] * 4
        + [pltpu.SemaphoreType.DMA((dp_count,))] * 2
        + [pltpu.SemaphoreType.DMA((ctx_count,))] * 2,
        compiler_params=pltpu.CompilerParams(
            collective_id=0, has_side_effects=True, vmem_limit_bytes=48 * 2**20
        ),
        name="delta_backward",
    )(queries, key_rows, value_rows, out_grad, columns, lines, hidden_in)
    return (dq, dk, dv, dgate.reshape(heads, tokens), own_grad.T)


def solution(mesh):
    rows = P(("dp", "ctx"), None)
    in_specs = (
        rows, rows, rows, rows, P(), P(None, ("dp", "ctx")), rows, P("dp", None), P(), P(),
    )
    out_specs = (rows, rows, rows, P(None, ("dp", "ctx")), rows)
    return jax.shard_map(local, mesh=mesh, in_specs=in_specs, out_specs=out_specs, check_vma=False)
```

```python
import functools

import jax
import jax.numpy as jnp
from jax import lax
from jax.experimental import pallas as pl
from jax.experimental.pallas import tpu as pltpu
from jax.sharding import PartitionSpec as P

PACK = 2
JOIN = 2
SMALL = 16
MESH = pl.DeviceIdType.MESH
F32 = jnp.float32
BF16 = jnp.bfloat16


def split(x):
    hi = x.astype(BF16)
    return hi, (x - hi.astype(F32)).astype(BF16)


def left(x):
    return jnp.concatenate(split(x), axis=1)


def left_t(x):
    return jnp.concatenate(split(x), axis=0)


def right(x):
    row = jnp.concatenate(split(x), axis=1)
    return jnp.concatenate([row, row], axis=0)


def right_t(x):
    hi, lo = split(x)
    return jnp.concatenate(
        [jnp.concatenate([hi, hi], axis=1), jnp.concatenate([lo, lo], axis=1)], axis=0
    )


def contract(a, b, dims):
    out = lax.dot_general(a, b, ((dims[:1], dims[1:]), ((), ())), preferred_element_type=F32)
    half = out.shape[1] // 2
    return out[:, :half] + out[:, half:]


def mul(a, b):
    return contract(left(a), right(b), (1, 0))


def mul_t(a, b):
    return contract(left(a), right_t(b), (1, 1))


def t_mul(a, b):
    return contract(left_t(a), right(b), (0, 0))


def stack(*parts):
    return jnp.concatenate(parts, axis=0)


def row_sum(x):
    return jnp.sum(x, axis=1, keepdims=True)


def inverses(lows, rows, cols):
    size = lows[0].shape[0]
    eye = jnp.where(rows == cols, 1.0, 0.0)
    base = min(SMALL, size)
    same = (rows // base) == (cols // base)
    powers = [jnp.where(same, -low, 0.0) for low in lows]
    totals = [eye + power for power in powers]
    powers = [mul(power, power) for power in powers]
    reach = 2
    while reach * 2 < base:
        both = [mul(stack(t, p), p) for t, p in zip(totals, powers)]
        totals = [t + b[:size] for t, b in zip(totals, both)]
        powers = [b[size:] for b in both]
        reach *= 2
    totals = [t + mul(t, p) for t, p in zip(totals, powers)]
    while base < size:
        own = ((rows // (2 * base)) == (cols // (2 * base))) & ((rows // base) != (cols // base))
        parts = [jnp.where(own, low, 0.0) for low in lows]
        mids = [mul(t, part) for t, part in zip(totals, parts)]
        totals = [t - mul(m, t) for t, m in zip(totals, mids)]
        base *= 2
    return totals


def kernel(
    q_ref, k_ref, v_ref, o_ref, cols_ref, rows_ref, hidden_ref,
    dq_ref, dk_ref, dv_ref, dgate_ref, weight_ref,
    inv_ref, mix_ref, dkk_ref, dec_ref, map_ref, fout_ref, bout_ref, fin_ref, bin_ref,
    dlogit_ref, whole_ref, near_out, near_in, far_out, far_in,
    fsend, frecv, bsend, brecv, nsend, nrecv, wsend, wrecv,
):
    tokens = q_ref.shape[0]
    groups = cols_ref.shape[0]
    width = fin_ref.shape[-1]
    count = lax.axis_size("ctx")
    seg = lax.axis_index("ctx")
    last = count - 1

    barrier = pltpu.get_barrier_semaphore()

    part = lax.axis_index("dp")
    parts = lax.axis_size("dp")
    for by in range(1, count):
        pl.semaphore_signal(
            barrier, inc=1, device_id={"ctx": lax.rem(seg + by, count)}, device_id_type=MESH
        )
    for by in range(1, parts):
        pl.semaphore_signal(
            barrier, inc=1, device_id={"dp": lax.rem(part + by, parts)}, device_id_type=MESH
        )
    pl.semaphore_wait(barrier, count + parts - 2)

    def forward_copy(group):
        return pltpu.make_async_remote_copy(
            src_ref=fout_ref.at[group], dst_ref=fin_ref.at[group],
            send_sem=fsend.at[group], recv_sem=frecv.at[group],
            device_id={"ctx": seg + 1}, device_id_type=MESH,
        )

    def backward_copy(group):
        return pltpu.make_async_remote_copy(
            src_ref=bout_ref.at[group], dst_ref=bin_ref.at[group],
            send_sem=bsend.at[group], recv_sem=brecv.at[group],
            device_id={"ctx": seg - 1}, device_id_type=MESH,
        )

    rows = lax.broadcasted_iota(jnp.int32, (tokens, tokens), 0)
    cols = lax.broadcasted_iota(jnp.int32, (tokens, tokens), 1)
    heads = range(PACK)
    batch = range(PACK * JOIN)

    def lanes(group, i):
        return pl.ds(pl.multiple_of((group * PACK + i) * width, width), width)

    def load(ref, group, i):
        return ref[:, lanes(group, i)].astype(F32)

    def token_columns(group, i):
        block = cols_ref[group + i // PACK]
        row_block = rows_ref[group + i // PACK]
        i = i % PACK
        beta = block[:, i:i + 1]
        gamma = block[:, PACK + i:PACK + i + 1]
        number = block[:, 2 * PACK:2 * PACK + 1]
        weight = block[:, 2 * PACK + 1:2 * PACK + 2]
        gamma_row = row_block[i:i + 1, :]
        number_row = row_block[PACK:PACK + 1, :]
        head = jnp.where(number == 0.0, jnp.exp(gamma), 0.0)
        tied = number == number_row[:, tokens - 1:tokens]
        tail = jnp.where(
            tied, jnp.exp(jnp.where(tied, gamma_row[:, tokens - 1:tokens] - gamma, 0.0)), 0.0
        )
        return beta, gamma, number, weight, gamma_row, number_row, head, tail

    def scales(x):
        return lax.rsqrt(row_sum(x * x) + 1e-06)

    def local_part(group):
        lows, keep = [], []
        for i in batch:
            beta, gamma, number, weight, gamma_row, number_row, head, tail = token_columns(group, i)
            q, k = load(q_ref, group, i), load(k_ref, group, i)
            qh, kh = q * scales(q), k * scales(k)
            linked = (number == number_row) & (rows >= cols)
            decay = jnp.where(linked, jnp.exp(jnp.where(linked, gamma - gamma_row, 0.0)), 0.0)
            both = mul_t(stack(kh, qh), kh)
            dkk = jnp.where(rows > cols, decay * both[:tokens], 0.0)
            mix = decay * both[tokens:]
            dec_ref[group + i // PACK, i % PACK] = decay
            dkk_ref[group + i // PACK, i % PACK] = dkk
            mix_ref[group + i // PACK, i % PACK] = mix
            lows.append(beta * dkk)
            keep.append((beta, weight, head, tail, qh, kh, mix))
        invs = inverses(lows, rows, cols)
        for i in batch:
            inv_ref[group + i // PACK, i % PACK] = invs[i]
        pairs = []
        for i in batch:
            beta, weight, head, tail, qh, kh, mix = keep[i]
            v = load(v_ref, group, i)
            pairs.append(mul(invs[i], jnp.concatenate([beta * v, (beta * head) * kh], axis=1)))
        eye = jnp.where(rows == cols, 1.0, 0.0)
        for i in batch:
            beta, weight, head, tail, qh, kh, mix = keep[i]
            z = pairs[i][:, width:]
            ends = t_mul(pairs[i], tail * kh)
            fout_ref[group + i // PACK, i % PACK] = ends[:width]
            map_ref[group + i // PACK, i % PACK] = head[tokens - 1:tokens, :] * eye - ends[width:]
            carry = head * qh - mul(mix, z)
            bout_ref[group + i // PACK, i % PACK] = t_mul(load(o_ref, group, i) * weight, carry)

    def forward_hop(group):
        @pl.when(seg == 0)
        def _():
            fin_ref[group] = jnp.zeros_like(fin_ref[group])

        @pl.when(seg > 0)
        def _():
            forward_copy(group).wait_recv()

        @pl.when((seg > 0) & (seg < last))
        def _():
            for i in heads:
                fout_ref[group, i] = fout_ref[group, i] + mul(fin_ref[group, i], map_ref[group, i])

        @pl.when(seg < last)
        def _():
            forward_copy(group).start()

    def backward_hop(group):
        @pl.when(seg == last)
        def _():
            bin_ref[group] = jnp.zeros_like(bin_ref[group])

        @pl.when(seg < last)
        def _():
            backward_copy(group).wait_recv()

        @pl.when((seg > 0) & (seg < last))
        def _():
            for i in heads:
                bout_ref[group, i] = bout_ref[group, i] + mul_t(bin_ref[group, i], map_ref[group, i])

        @pl.when(seg > 0)
        def _():
            backward_copy(group).start()

    def gradient_part(group):
        upper = jnp.where(rows < cols, 1.0, 0.0).astype(BF16)
        upper = stack(upper, upper)
        keep = []
        for i in batch:
            beta, gamma, number, weight, gamma_row, number_row, head, tail = token_columns(group, i)
            q, k = load(q_ref, group, i), load(k_ref, group, i)
            qs, ks = scales(q), scales(k)
            qh, kh = q * qs, k * ks
            state = fin_ref[group + i // PACK, i % PACK]
            both = mul_t(stack(qh, kh), state)
            keep.append((beta, weight, head, tail, qs, ks, qh, kh, state, both[:tokens], both[tokens:]))
        rests = [load(v_ref, group, i) - keep[i][2] * keep[i][10] for i in batch]
        us = [mul(inv_ref[group + i // PACK, i % PACK], keep[i][0] * rests[i]) for i in batch]
        dos = [load(o_ref, group, i) * keep[i][1] for i in batch]
        dus = [
            t_mul(mix_ref[group + i // PACK, i % PACK], dos[i]) + mul_t(keep[i][3] * keep[i][7], bin_ref[group + i // PACK, i % PACK])
            for i in batch
        ]
        drs = [t_mul(inv_ref[group + i // PACK, i % PACK], dus[i]) for i in batch]
        squares = [mul_t(stack(dos[i], drs[i]), us[i]) for i in batch]
        logit_columns = []
        for i in batch:
            beta, weight, head, tail, qs, ks, qh, kh, state, qstate, kstate = keep[i]
            u, do, dr, rest, after = us[i], dos[i], drs[i], rests[i], bin_ref[group + i // PACK, i % PACK]
            decay, dkk = dec_ref[group + i // PACK, i % PACK], dkk_ref[group + i // PACK, i % PACK]
            dmix = squares[i][:tokens]
            dlow = jnp.where(rows > cols, -squares[i][tokens:], 0.0)
            inward = mul(stack(head * do, (-beta * head) * dr), state)
            uafter = mul(u, after)
            da = dmix * decay
            dpair = dlow * (beta * decay)
            pairs = stack(da, dpair)
            direct = mul(pairs, kh)
            turned = t_mul(pairs, stack(qh, kh))
            dqh = inward[:tokens] + direct[:tokens]
            dkh = inward[tokens:] + direct[tokens:] + turned + tail * uafter
            dq_ref[:, lanes(group, i)] = (qs * (dqh - qh * row_sum(qh * dqh))).astype(BF16)
            dk_ref[:, lanes(group, i)] = (ks * (dkh - kh * row_sum(kh * dkh))).astype(BF16)
            dv_ref[:, lanes(group, i)] = (beta * dr).astype(BF16)
            lowpart = dlow * dkk
            spread = dmix * mix_ref[group + i // PACK, i % PACK] + beta * lowpart
            across = lax.dot_general(
                left(spread), upper, (((1,), (0,)), ((), ())), preferred_element_type=F32
            )
            total = jnp.sum(row_sum(after * state), axis=0, keepdims=True)
            headgrad = row_sum(do * qstate) - beta * row_sum(dr * kstate)
            headgrad = head * (headgrad + jnp.where(rows[:, :1] == tokens - 1, total, 0.0))
            tailgrad = tail * row_sum(kh * uafter)
            dgate_ref[group + i // PACK, i % PACK:i % PACK + 1, :] = jnp.sum(
                jnp.where(rows >= cols, across + headgrad, tailgrad), axis=0, keepdims=True
            )
            dbeta = row_sum(dr * rest) + row_sum(lowpart)
            logit_columns.append(dbeta * beta * (1.0 - beta))
        for j in range(JOIN):
            dlogit_ref[group + j] = jnp.concatenate(
                logit_columns[j * PACK:(j + 1) * PACK], axis=1
            )

    def step(t, unused):
        @pl.when((t < groups) & (lax.rem(t, JOIN) == 0))
        def _():
            local_part(t)

        f = t - seg

        @pl.when((f >= 0) & (f < groups))
        def _():
            forward_hop(f)

        b = t - (last - seg)

        @pl.when((b >= 0) & (b < groups))
        def _():
            backward_hop(b)

        done = t - last + 1

        @pl.when((done > 0) & (lax.rem(done, JOIN) == 0))
        def _():
            gradient_part(done - JOIN)

        return unused

    lax.fori_loop(0, groups + last, step, 0)

    def drain(group, unused):
        @pl.when(seg < last)
        def _():
            forward_copy(group).wait_send()

        @pl.when(seg > 0)
        def _():
            backward_copy(group).wait_send()

        return unused

    logit_grad = jnp.concatenate([dlogit_ref[g] for g in range(groups)], axis=1)
    hidden = hidden_ref[...]
    whole_ref[...] = lax.dot_general(
        left_t(logit_grad), stack(hidden, hidden), (((0,), (0,)), ((), ())),
        preferred_element_type=F32,
    )
    owned = near_out.shape[-1]
    for p in range(parts):
        for c in range(count):
            at = (p * count + c) * owned
            near_out[p, c] = whole_ref[:, at:at + owned]

    def near_copy(by):
        to = lax.rem(part + by, parts)
        return pltpu.make_async_remote_copy(
            src_ref=near_out.at[to], dst_ref=near_in.at[by - 1],
            send_sem=nsend.at[by - 1], recv_sem=nrecv.at[by - 1],
            device_id={"dp": to}, device_id_type=MESH,
        )

    def far_copy(by):
        to = lax.rem(seg + by, count)
        return pltpu.make_async_remote_copy(
            src_ref=far_out.at[to], dst_ref=far_in.at[by - 1],
            send_sem=wsend.at[by - 1], recv_sem=wrecv.at[by - 1],
            device_id={"ctx": to}, device_id_type=MESH,
        )

    for by in range(1, parts):
        near_copy(by).start()
    total = near_out[part]
    for by in range(1, parts):
        near_copy(by).wait_recv()
        total = total + near_in[by - 1]
    far_out[...] = total
    for by in range(1, count):
        far_copy(by).start()
    total = far_out[seg]
    for by in range(1, count):
        far_copy(by).wait_recv()
        total = total + far_in[by - 1]
    weight_ref[...] = total
    for by in range(1, parts):
        near_copy(by).wait_send()
    for by in range(1, count):
        far_copy(by).wait_send()

    lax.fori_loop(0, groups, drain, 0)


def token_plan(row_lengths, positions):
    ends = jnp.cumsum(row_lengths)
    begins = ends - row_lengths
    starts = jnp.any(positions[:, None] == begins[None, :], axis=1).astype(jnp.float32)
    member = (
        (positions[:, None] >= begins[None, :]) & (positions[:, None] < ends[None, :])
    ).astype(jnp.float32)
    return (starts, member)


def advantages(rewards, prompts):
    same = (prompts[:, None] == prompts[None, :]).astype(jnp.float32)
    return rewards - jnp.sum(same * rewards[None, :], axis=1) / jnp.sum(same, axis=1)


def local(
    queries, key_rows, value_rows, hidden_in, beta_weight, log_gate, out_grad,
    lengths, rewards, prompts,
):
    tokens = queries.shape[0]
    heads = beta_weight.shape[1]
    width = queries.shape[1] // heads
    groups = heads // PACK
    ctx_count = lax.axis_size("ctx")
    roll_count = lengths.shape[1]
    group_tokens = tokens * ctx_count
    positions = lax.axis_index("ctx") * tokens + jnp.arange(tokens, dtype=jnp.int32)
    starts, member = token_plan(lengths[0], positions)
    own_advantage = lax.dynamic_slice_in_dim(
        advantages(rewards, prompts), lax.axis_index("dp") * roll_count, roll_count
    )
    roll_weight = own_advantage * group_tokens / (roll_count * lengths[0].astype(jnp.float32))
    token_weight = jnp.sum(member * roll_weight[None, :], axis=-1)
    logits = jnp.dot(hidden_in, beta_weight, preferred_element_type=jnp.float32)
    beta = jax.nn.sigmoid(logits)
    gamma = jnp.cumsum(log_gate, axis=-1)
    number = jnp.cumsum(starts)
    shared = jnp.broadcast_to(
        jnp.stack([number, token_weight], axis=1)[None], (groups, tokens, 2)
    )
    columns = jnp.concatenate(
        [
            beta.reshape(tokens, groups, PACK).transpose(1, 0, 2),
            gamma.reshape(groups, PACK, tokens).transpose(0, 2, 1),
            shared,
        ],
        axis=2,
    )
    lines = jnp.concatenate(
        [
            gamma.reshape(groups, PACK, tokens),
            jnp.broadcast_to(number[None, None], (groups, 1, tokens)),
        ],
        axis=1,
    )
    square = (groups, PACK, tokens, tokens)
    states = (groups, PACK, width, width)
    vmem = pl.BlockSpec(memory_space=pltpu.VMEM)
    model = hidden_in.shape[1]
    dp_count = lax.axis_size("dp")
    owned = model // (dp_count * ctx_count)
    dq, dk, dv, dgate, own_grad = pl.pallas_call(
        kernel,
        out_shape=(
            jax.ShapeDtypeStruct(queries.shape, BF16),
            jax.ShapeDtypeStruct(queries.shape, BF16),
            jax.ShapeDtypeStruct(queries.shape, BF16),
            jax.ShapeDtypeStruct((groups, PACK, tokens), F32),
            jax.ShapeDtypeStruct((heads, owned), F32),
        ),
        in_specs=[vmem] * 7,
        out_specs=(vmem,) * 5,
        scratch_shapes=[pltpu.VMEM(square, F32)] * 4
        + [pltpu.VMEM(states, F32)] * 5
        + [
            pltpu.VMEM((groups, tokens, PACK), F32),
            pltpu.VMEM((heads, model), F32),
            pltpu.VMEM((dp_count, ctx_count, heads, owned), F32),
            pltpu.VMEM((dp_count - 1 or 1, ctx_count, heads, owned), F32),
            pltpu.VMEM((ctx_count, heads, owned), F32),
            pltpu.VMEM((ctx_count - 1, heads, owned), F32),
        ]
        + [pltpu.SemaphoreType.DMA((groups,))] * 4
        + [pltpu.SemaphoreType.DMA((dp_count,))] * 2
        + [pltpu.SemaphoreType.DMA((ctx_count,))] * 2,
        compiler_params=pltpu.CompilerParams(
            collective_id=0, has_side_effects=True, vmem_limit_bytes=48 * 2**20
        ),
        name="delta_backward",
    )(queries, key_rows, value_rows, out_grad, columns, lines, hidden_in)
    return (dq, dk, dv, dgate.reshape(heads, tokens), own_grad.T)


def solution(mesh):
    rows = P(("dp", "ctx"), None)
    in_specs = (
        rows, rows, rows, rows, P(), P(None, ("dp", "ctx")), rows, P("dp", None), P(), P(),
    )
    out_specs = (rows, rows, rows, P(None, ("dp", "ctx")), rows)
    return jax.shard_map(local, mesh=mesh, in_specs=in_specs, out_specs=out_specs, check_vma=False)
```
